32 devices in a mesh: row: 4 (over y, x), sa: 4 (over z), ha: 2 (over core).
Axes of the slice: x: 2, y: 2, z: 4, core: 2. Of those that a mesh axis runs over, the one named last changes fastest.
Arguments:
- records: float32 [64, 16, 8192], P(None, 'sa', ('row', 'ha')), parts along dimension 2, may hold values from -6 to 6
- halo_mass: float32 [16, 8192], P('sa', ('row', 'ha')), parts along dimension 1, may hold values from 0.1 to 10
- forest_id: int32 [16, 8192], P('sa', ('row', 'ha')), parts along dimension 1, may hold values from 0 to 1023, as said below
- dest_block: int32 [16, 8192], P('sa', ('row', 'ha')), parts along dimension 1, may hold values from 0 to 319, as said below
- dest_slot: int32 [16, 8192], P('sa', ('row', 'ha')), parts along dimension 1, may hold values from 0 to 127
Outputs:
- blocks: float32 [64, 1280, 128], P(None, ('row', 'sa', 'ha')), parts along dimension 1
- block_mass: float32 [1280, 128], P(('row', 'sa', 'ha')), parts along dimension 0
- forest_mass: float32 [4096], P(('row', 'sa', 'ha')), parts along dimension 0
- forest_mean: float32 [64, 4096], P(None, ('row', 'sa', 'ha')), parts along dimension 1
- forest_second: float32 [64, 4096], P(None, ('row', 'sa', 'ha')), parts along dimension 1
The draws below stay inside these ranges and needn't reach their ends.
There are 4 independent parts, one for each index of `row`. The reference program is written for one: setup_inputs(seed, part) draws one part's arguments, and reference() takes and returns one part's arrays. A program takes and returns all parts, laid end to end along the dimension named above; each array names one. Nothing has to cross between parts.
Inputs may be any that keep to these rules, and one draw needn't show every extreme that they name: The pairs (dest_block, dest_slot) are distinct over all halos. Block b lies on the device of index b // 40 of sa+ha (sa slowest), and forest f is owned by the device of index f // 128; every halo goes to a block of its forest's owner. On each device the used slots are the first ones in block-then-slot order, and every forest has at least one halo. `forest_id`: of the halos of one device (one index of sa and one of ha), at most 704 go to blocks of one device; in every draw some pair of devices reaches 704, and some device has all its 5120 slots used.
All inputs are finite; a program needn't handle non-finite values.
Results may differ from the reference program's by a relative error of at most 0.0003.
Values sent between devices are 32-bit elements; how exact they have to be, the bound alone decides.
A program may use at most 64 MiB of HBM per device.

```python
import math
import jax
import jax.numpy as jnp
from jax import lax

FIELDS = 64
S_DEV = 4
H_DEV = 1024
FOR_DEV = 128
SNAPS = 16
HALOS = 2048
BLK_DEV = 40
NBLK = 320
NFOR = 1024
N_SA = 4
N_HA = 2


def route_table(key):
    peer_count = N_SA * N_HA
    local_count = S_DEV * H_DEV
    pair_mean = local_count // peer_count
    entries_all = peer_count * local_count
    slots_dev = BLK_DEV * 128
    half_peers = peer_count // 2
    key_list = jax.random.split(jax.random.fold_in(key, 91), 8)
    lift_up = jax.random.randint(key_list[0], (half_peers,), 0, pair_mean // 4 + 1)
    lift_up = lift_up.at[0].set(pair_mean // 4)
    load_in = pair_mean + jnp.concatenate([lift_up, -lift_up])[jax.random.permutation(key_list[1], peer_count)]
    wobble = jax.random.randint(key_list[2], (half_peers,), -(pair_mean // 8), pair_mean // 8 + 1)
    wobble = wobble.at[0].set(pair_mean // 8)
    offsets = jnp.concatenate([wobble, -wobble])
    shift_dst = jax.random.permutation(key_list[3], peer_count)
    shift_src = jax.random.permutation(key_list[4], peer_count)
    pair_counts = load_in[None, :] + offsets[(shift_dst[None, :] - shift_src[:, None]) % peer_count]
    flat_counts = pair_counts.T.reshape(-1)
    pair_ends = jnp.cumsum(flat_counts).astype(jnp.int32)
    entry_index = jnp.arange(entries_all, dtype=jnp.int32)
    pair_of = jnp.searchsorted(pair_ends, entry_index, side='right').astype(jnp.int32)
    dest_dev = pair_of // peer_count
    src_dev = pair_of % peer_count
    inbound = (peer_count * load_in).astype(jnp.int32)
    recv_start = (jnp.cumsum(inbound) - inbound).astype(jnp.int32)
    shuffle_in = jax.random.permutation(key_list[5], entries_all).astype(jnp.int32)
    order_in = jnp.argsort(dest_dev * entries_all + shuffle_in, stable=True)
    place_in = jnp.zeros((entries_all,), jnp.int32).at[order_in].set(entry_index)
    position = place_in - recv_start[dest_dev]
    shuffle_out = jax.random.permutation(key_list[6], entries_all).astype(jnp.int32)
    order_out = jnp.argsort(src_dev * entries_all + shuffle_out, stable=True)
    place_out = jnp.zeros((entries_all,), jnp.int32).at[order_out].set(entry_index)
    local_pos = place_out - src_dev * local_count
    heights = jax.random.randint(key_list[7], (peer_count, FOR_DEV), 1, 8) ** 2
    climb_sum = jnp.cumsum(heights, axis=1)
    spare_slots = inbound - FOR_DEV
    starts = jnp.arange(FOR_DEV, dtype=jnp.int32)[None, :] + spare_slots[:, None] * (climb_sum - heights) // climb_sum[:, -1:]
    global_starts = (recv_start[:, None] + starts).reshape(-1).astype(jnp.int32)
    forest = (jnp.searchsorted(global_starts, place_in, side='right') - 1).astype(jnp.int32)
    global_slot = dest_dev * slots_dev + position
    snap_index = src_dev // N_HA * S_DEV + local_pos // H_DEV
    halo_index = src_dev % N_HA * H_DEV + local_pos % H_DEV

    def spread(values):
        return jnp.zeros((SNAPS, HALOS), jnp.int32).at[snap_index, halo_index].set(values.astype(jnp.int32))
    return (spread(forest), spread(global_slot // 128), spread(global_slot % 128))


def draw_forest_id(key, part):
    return route_table(key)[0]


def draw_dest_block(key, part):
    return route_table(key)[1]


def draw_dest_slot(key, part):
    return route_table(key)[2]


def block_levels(stream_key, extent, cuts, least, high):
    def one(dim, shards_of):
        steps = jax.random.uniform(jax.random.fold_in(jax.random.fold_in(stream_key, 6), dim), (shards_of,), jnp.float32, least / len(cuts), high / len(cuts))
        return jnp.repeat(jnp.exp(steps), extent[dim] // shards_of).reshape((-1,) + (1,) * (len(extent) - dim - 1))

    loudness = one(*cuts[0])
    for cut in cuts[1:]:
        loudness = loudness * one(*cut)
    return loudness


def centred(key, extent, scale, most, pieces=(), kind=jnp.bfloat16):
    values = jax.random.normal(key, extent, jnp.float32) * scale
    if len(pieces) > 0:
        values = block_levels(key, extent, pieces, -0.22, 0.18) * values
    return jnp.clip(values, min=-most, max=most).astype(kind)


def setup_inputs(seed: int = 0, part: int = 0) -> dict:
    keys = jax.random.split(jax.random.key(seed), 6)
    part_splits = jax.random.split(jax.random.fold_in(keys[5], part), 6)
    return {
        "records": centred(part_splits[0], (FIELDS, SNAPS, HALOS), 1.0, 6.0, ((1, 4), (2, 2)), jnp.float32),
        "halo_mass": jnp.clip(jnp.exp(math.log(10.0) - 4.6051702 * jax.random.uniform(part_splits[1], (SNAPS, HALOS), jnp.float32) ** block_levels(part_splits[1], (SNAPS, HALOS), ((0, 4), (1, 2)), -0.2, 0.2)), 0.1, 10.0),
        "forest_id": draw_forest_id(jax.random.fold_in(jax.random.fold_in(keys[5], part), 71), part),
        "dest_block": draw_dest_block(jax.random.fold_in(jax.random.fold_in(keys[5], part), 71), part),
        "dest_slot": draw_dest_slot(jax.random.fold_in(jax.random.fold_in(keys[5], part), 71), part),
    }


def reference(records, halo_mass, forest_id, dest_block, dest_slot):
    fields = records.shape[0]
    flat = records.reshape(fields, -1)
    weights_in = halo_mass.reshape(-1)
    home = (dest_block * 128 + dest_slot).reshape(-1).astype(jnp.int32)
    slot_total = NBLK * 128
    blocks = jnp.zeros((fields, slot_total), jnp.float32).at[:, home].set(flat)
    block_mass = jnp.zeros((slot_total,), jnp.float32).at[home].set(weights_in)
    forest_in = forest_id.reshape(-1).astype(jnp.int32)
    weight = jax.ops.segment_sum(weights_in, forest_in, NFOR)

    def per_field(values):
        scaled = weights_in * values
        return (jax.ops.segment_sum(scaled, forest_in, NFOR),
                jax.ops.segment_sum(scaled * values, forest_in, NFOR))

    first_sum, square_sum = lax.map(per_field, flat)
    mass_total = jnp.sum(weights_in)
    forest_mass = weight * (NFOR / mass_total)
    return (blocks.reshape(fields, NBLK, 128), block_mass.reshape(NBLK, 128),
            forest_mass, first_sum / weight[None, :], square_sum / weight[None, :])
```

```python
import functools

import jax
import jax.numpy as jnp
from jax import lax
from jax.experimental import pallas as pl
from jax.experimental.pallas import tpu as pltpu
from jax.sharding import PartitionSpec as P

FOR_DEV = 128
BLK_DEV = 40
LANES = 128
LABELS = 4


def round_up(value, unit):
    return (value + unit - 1) // unit * unit


class Plan:
    def __init__(self, fields, snaps, halos, peers):
        self.fields, self.snaps, self.halos, self.peers = fields, snaps, halos, peers
        self.local = snaps * halos
        self.tiles = self.local // LANES
        self.chunks = halos // LANES
        capacity = 11 * (self.local // peers) // 8
        self.cap = round_up(capacity, 16)
        self.half = self.cap // 2
        self.groups = LANES // LABELS
        self.lab_rows = round_up((self.cap + self.groups - 1) // self.groups, 8)
        self.rows = self.half + self.lab_rows
        self.slots = BLK_DEV * LANES
        self.per_tile = LANES // self.lab_rows
        self.lab_tiles = (peers + self.per_tile - 1) // self.per_tile
        assert 2 * fields == LANES


def pack_kernel(plan, rec_ref, mass_ref, forest_ref, block_ref, slot_ref, out_ref,
                rows_in, rows_out, flat, members, target, target_s, sem):
    snaps, fields, peers, tiles = plan.snaps, plan.fields, plan.peers, plan.tiles
    for chunk in range(plan.chunks):
        here = pl.ds(chunk * snaps, snaps)
        cut = pl.ds(chunk * LANES, LANES)
        flat[0, here, :] = block_ref[:, cut].astype(jnp.float32)
        flat[1, here, :] = slot_ref[:, cut].astype(jnp.float32)
        flat[2, here, :] = forest_ref[:, cut].astype(jnp.float32)
        flat[3, here, :] = mass_ref[:, cut]
    block = flat[0]
    mass = flat[3]
    for owner in range(peers):
        inside = (block >= owner * BLK_DEV) & (block < (owner + 1) * BLK_DEV)
        members[pl.ds(owner * tiles, tiles), :] = jnp.where(inside, 1.0, 0.0).astype(jnp.bfloat16)
    down = lax.broadcasted_iota(jnp.int32, (LANES, LANES), 0)
    across = lax.broadcasted_iota(jnp.int32, (LANES, LANES), 1)
    upper = jnp.where(down < across, 1.0, 0.0).astype(jnp.bfloat16)
    every = jnp.ones((LANES, LANES), jnp.bfloat16)
    lower = jnp.where(
        lax.broadcasted_iota(jnp.int32, (tiles, tiles), 0)
        > lax.broadcasted_iota(jnp.int32, (tiles, tiles), 1), 1.0, 0.0).astype(jnp.bfloat16)
    place = jnp.zeros((tiles, LANES), jnp.float32)
    owner_of = jnp.zeros((tiles, LANES), jnp.float32)
    for owner in range(peers):
        member = members[pl.ds(owner * tiles, tiles), :]
        within = jnp.dot(member, upper, preferred_element_type=jnp.float32)
        totals = jnp.dot(member, every, preferred_element_type=jnp.float32).astype(jnp.bfloat16)
        before = jnp.dot(lower, totals, preferred_element_type=jnp.float32)
        chosen = member.astype(jnp.float32)
        place = place + chosen * (within + before + float(owner * plan.cap))
        owner_of = owner_of + chosen * float(owner)
    target[...] = place.astype(jnp.int32)
    copy = pltpu.make_async_copy(target, target_s, sem)
    copy.start()
    flat[1] = (block - owner_of * float(BLK_DEV)) * float(LANES) + flat[1]
    flat[2] = flat[2] - owner_of * float(FOR_DEV)
    total = jnp.sum(mass)

    sub = lax.broadcasted_iota(jnp.int32, (8, LANES), 0)
    zeros = jnp.zeros((LANES - fields - 8, LANES), jnp.float32)
    for chunk in range(plan.chunks):
        for snap in range(snaps):
            row = chunk * snaps + snap
            values = rec_ref[:, snap, pl.ds(chunk * LANES, LANES)]
            label = jnp.where(sub == 0, flat[3, pl.ds(row, 1), :], total)
            label = jnp.where(sub == 1, flat[1, pl.ds(row, 1), :], label)
            label = jnp.where(sub == 2, flat[2, pl.ds(row, 1), :], label)
            whole = jnp.concatenate([values, label, zeros], axis=0)
            rows_in[pl.ds(row * LANES, LANES), :] = whole.T

    lane = lax.broadcasted_iota(jnp.int32, (8, LANES), 1)
    empty = jnp.where(lane == fields + 1, float(plan.slots),
                      jnp.where(lane == fields + 3, total, 0.0))

    def clear(step, carry):
        for part in range(8):
            rows_out[pl.ds(pl.multiple_of(step * 64 + part * 8, 8), 8), :] = empty
        return carry

    lax.fori_loop(0, peers * plan.cap // 64, clear, 0)
    copy.wait()

    def scatter(row, carry):
        for col in range(LANES):
            to = target_s[row, col]
            rows_out[pl.ds(to, 1), :] = rows_in[pl.ds(row * LANES + col, 1), :]
        return carry

    lax.fori_loop(0, tiles, scatter, 0)

    def squeeze(peer, carry):
        start = peer * plan.cap
        for step in range(plan.half // 8):
            low = rows_out[pl.ds(pl.multiple_of(start + step * 8, 8), 8), :]
            high = rows_out[pl.ds(pl.multiple_of(start + plan.half + step * 8, 8), 8), :]
            out_ref[peer, pl.ds(step * 8, 8), :] = jnp.where(
                lane < fields, low, pltpu.roll(high, fields, 1))
        per = plan.lab_rows // 8
        for part in range(per):
            gathered = jnp.zeros((8, LANES), jnp.float32)
            for group in range(plan.groups):
                tile = group * per + part
                if tile * 8 < plan.cap:
                    piece = rows_out[pl.ds(pl.multiple_of(start + tile * 8, 8), 8), :]
                    moved = pltpu.roll(piece, (group * LABELS - fields) % LANES, 1)
                    gathered = jnp.where(lane // LABELS == group, moved, gathered)
            out_ref[peer, pl.ds(plan.half + part * 8, 8), :] = gathered
        return carry

    lax.fori_loop(0, peers, squeeze, 0)


def exchange_kernel(plan, n_ha, send_ref, recv_ref, send_sem, recv_sem, own_sem):
    peers = plan.peers
    me = lax.axis_index("sa") * n_ha + lax.axis_index("ha")
    barrier = pltpu.get_barrier_semaphore()

    def where_is(peer):
        return {"sa": peer // n_ha, "ha": lax.rem(peer, n_ha)}

    for step in range(1, peers):
        pl.semaphore_signal(barrier, inc=1, device_id=where_is(lax.rem(me + step, peers)),
                            device_id_type=pl.DeviceIdType.MESH)
    pl.semaphore_wait(barrier, peers - 1)
    copies = []
    for step in range(1, peers):
        peer = lax.rem(me + step, peers)
        copy = pltpu.make_async_remote_copy(
            src_ref=send_ref.at[peer],
            dst_ref=recv_ref.at[me],
            send_sem=send_sem.at[step],
            recv_sem=recv_sem.at[step],
            device_id=where_is(peer),
            device_id_type=pl.DeviceIdType.MESH,
        )
        copy.start()
        copies.append(copy)
    own = pltpu.make_async_copy(send_ref.at[me], recv_ref.at[me], own_sem)
    own.start()
    own.wait()
    for copy in copies:
        copy.wait()


def unpack_kernel(plan, got_ref, blocks_ref, mass_ref, fmass_ref, mean_ref, second_ref,
                  arrived, placed, labels, labels_s, sems):
    fields, peers = plan.fields, plan.peers
    per = plan.lab_rows // 8
    lane = lax.broadcasted_iota(jnp.int32, (8, LANES), 1)
    copies = []
    for tile in range(plan.lab_tiles):
        first = tile * plan.per_tile
        count = min(plan.per_tile, peers - first)
        pieces = [got_ref[first + k, pl.ds(plan.half, plan.lab_rows), :] for k in range(count)]
        rest = LANES - count * plan.lab_rows
        if rest:
            pieces.append(jnp.zeros((rest, LANES), jnp.float32))
        labels[tile] = jnp.concatenate(pieces, axis=0).T.astype(jnp.int32)
        copy = pltpu.make_async_copy(labels.at[tile], labels_s.at[tile], sems.at[tile])
        copy.start()
        copies.append(copy)

    def clear(step, carry):
        for part in range(8):
            placed[pl.ds(pl.multiple_of(step * 64 + part * 8, 8), 8), :] = jnp.zeros(
                (8, LANES), jnp.float32)
        return carry

    lax.fori_loop(0, plan.slots // 64, clear, 0)
    in_labels = (lane >= fields) & (lane < fields + LABELS)

    def spread(peer, carry):
        start = peer * plan.cap
        for step in range(plan.half // 8):
            both = got_ref[peer, pl.ds(step * 8, 8), :]
            for side in range(2):
                tile = side * (plan.half // 8) + step
                group, part = tile // per, tile % per
                label = got_ref[peer, pl.ds(plan.half + part * 8, 8), :]
                label = pltpu.roll(label, (fields - group * LABELS) % LANES, 1)
                record = both if side == 0 else pltpu.roll(both, fields, 1)
                arrived[pl.ds(pl.multiple_of(start + tile * 8, 8), 8), :] = jnp.where(
                    lane < fields, record, jnp.where(in_labels, label, 0.0))
        return carry

    lax.fori_loop(0, peers, spread, 0)
    for copy in copies:
        copy.wait()

    for peer in range(peers):
        tile, offset = peer // plan.per_tile, peer % plan.per_tile * plan.lab_rows
        whole = plan.cap // plan.lab_rows

        def scatter(group, carry, rows=plan.lab_rows, peer=peer, tile=tile, offset=offset):
            for row in range(rows):
                to = labels_s[tile, group * LABELS + 1, offset + row]
                placed[pl.ds(to, 1), :] = arrived[
                    pl.ds(peer * plan.cap + group * plan.lab_rows + row, 1), :]
            return carry

        lax.fori_loop(0, whole, scatter, 0)
        if plan.cap % plan.lab_rows:
            scatter(whole, 0, rows=plan.cap % plan.lab_rows)

    total = jnp.zeros((1, 1), jnp.float32)
    for peer in range(peers):
        total = total + arrived[pl.ds(peer * plan.cap, 1), :][:, fields + 3:fields + 4]
    forests = lax.broadcasted_iota(jnp.int32, (FOR_DEV, LANES), 0).astype(jnp.float32)
    wide = lax.broadcasted_iota(jnp.int32, (LANES, LANES), 1)

    def one_block(block, carry):
        sums, weights = carry
        rows = placed[pl.ds(pl.multiple_of(block * LANES, LANES), LANES), :]
        turned = rows.T
        blocks_ref[pl.ds(block, fields, stride=BLK_DEV), :] = turned[:fields]
        mass_row = turned[fields:fields + 1]
        mass_ref[pl.ds(block, 1), :] = mass_row
        hit = turned[fields + 2:fields + 3] == forests
        weights = weights + jnp.where(hit, mass_row, 0.0)
        member = jnp.where(hit, 1.0, 0.0).astype(jnp.bfloat16)
        mass = rows[:, fields:fields + 1]
        value = jnp.where(wide < fields, rows, pltpu.roll(rows, fields, 1))
        scaled = mass * value
        scaled = jnp.where(wide < fields, scaled, scaled * value)
        high = scaled.astype(jnp.bfloat16)
        low = (scaled - high.astype(jnp.float32)).astype(jnp.bfloat16)
        sums = sums + jnp.dot(member, high, preferred_element_type=jnp.float32)
        sums = sums + jnp.dot(member, low, preferred_element_type=jnp.float32)
        return sums, weights

    zero = jnp.zeros((FOR_DEV, LANES), jnp.float32)
    sums, weights = lax.fori_loop(0, BLK_DEV, one_block, (zero, zero))
    weight = jnp.sum(weights.T, axis=0, keepdims=True)
    sums = sums.T
    fmass_ref[...] = weight * (float(FOR_DEV * peers) / total)
    mean_ref[...] = sums[:fields] / weight
    second_ref[...] = sums[fields:] / weight


def on_device(n_ha, peers, records, halo_mass, forest_id, dest_block, dest_slot):
    fields, snaps, halos = records.shape
    plan = Plan(fields, snaps, halos, peers)
    f32, i32 = jnp.float32, jnp.int32
    vmem = pl.BlockSpec(memory_space=pltpu.VMEM)
    big = pltpu.CompilerParams(vmem_limit_bytes=48 * 1024 * 1024)
    send = pl.pallas_call(
        functools.partial(pack_kernel, plan),
        out_shape=jax.ShapeDtypeStruct((peers, plan.rows, LANES), f32),
        in_specs=[vmem] * 5,
        out_specs=vmem,
        scratch_shapes=[
            pltpu.VMEM((plan.local, LANES), f32),
            pltpu.VMEM((peers * plan.cap, LANES), f32),
            pltpu.VMEM((4, plan.tiles, LANES), f32),
            pltpu.VMEM((peers * plan.tiles, LANES), jnp.bfloat16),
            pltpu.VMEM((plan.tiles, LANES), i32),
            pltpu.SMEM((plan.tiles, LANES), i32),
            pltpu.SemaphoreType.DMA,
        ],
        compiler_params=big,
        name="pack",
    )(records, halo_mass, forest_id, dest_block, dest_slot)
    got = pl.pallas_call(
        functools.partial(exchange_kernel, plan, n_ha),
        out_shape=jax.ShapeDtypeStruct(send.shape, f32),
        in_specs=[pl.BlockSpec(memory_space=pl.ANY)],
        out_specs=pl.BlockSpec(memory_space=pl.ANY),
        scratch_shapes=[
            pltpu.SemaphoreType.DMA((peers,)),
            pltpu.SemaphoreType.DMA((peers,)),
            pltpu.SemaphoreType.DMA,
        ],
        compiler_params=pltpu.CompilerParams(collective_id=0, has_side_effects=True),
        name="exchange",
    )(send)
    blocks, block_mass, forest_mass, mean, second = pl.pallas_call(
        functools.partial(unpack_kernel, plan),
        out_shape=(
            jax.ShapeDtypeStruct((fields * BLK_DEV, LANES), f32),
            jax.ShapeDtypeStruct((BLK_DEV, LANES), f32),
            jax.ShapeDtypeStruct((1, FOR_DEV), f32),
            jax.ShapeDtypeStruct((fields, FOR_DEV), f32),
            jax.ShapeDtypeStruct((fields, FOR_DEV), f32),
        ),
        in_specs=[vmem],
        out_specs=(vmem,) * 5,
        scratch_shapes=[
            pltpu.VMEM((peers * plan.cap, LANES), f32),
            pltpu.VMEM((plan.slots + 8, LANES), f32),
            pltpu.VMEM((plan.lab_tiles, LANES, LANES), i32),
            pltpu.SMEM((plan.lab_tiles, LANES, LANES), i32),
            pltpu.SemaphoreType.DMA((plan.lab_tiles,)),
        ],
        compiler_params=big,
        name="unpack",
    )(got)
    return (
        blocks.reshape(fields, BLK_DEV, LANES),
        block_mass,
        forest_mass.reshape(FOR_DEV),
        mean,
        second,
    )


def solution(mesh):
    n_ha = mesh.shape["ha"]
    peers = mesh.shape["sa"] * n_ha
    in_specs = (
        P(None, "sa", ("row", "ha")),
        P("sa", ("row", "ha")),
        P("sa", ("row", "ha")),
        P("sa", ("row", "ha")),
        P("sa", ("row", "ha")),
    )
    out_specs = (
        P(None, ("row", "sa", "ha"), None),
        P(("row", "sa", "ha"), None),
        P(("row", "sa", "ha")),
        P(None, ("row", "sa", "ha")),
        P(None, ("row", "sa", "ha")),
    )
    return jax.shard_map(
        functools.partial(on_device, n_ha, peers),
        mesh=mesh, in_specs=in_specs, out_specs=out_specs, check_vma=False
    )
```

```python
import functools

import jax
import jax.numpy as jnp
from jax import lax
from jax.experimental import pallas as pl
from jax.experimental.pallas import tpu as pltpu
from jax.sharding import PartitionSpec as P

FOR_DEV = 128
BLK_DEV = 40
LANES = 128
LABELS = 4


def round_up(value, unit):
    return (value + unit - 1) // unit * unit


class Plan:
    def __init__(self, fields, snaps, halos, peers):
        self.fields, self.snaps, self.halos, self.peers = fields, snaps, halos, peers
        self.local = snaps * halos
        self.tiles = self.local // LANES
        self.chunks = halos // LANES
        capacity = 11 * (self.local // peers) // 8
        self.cap = round_up(capacity, 16)
        self.half = self.cap // 2
        self.groups = LANES // LABELS
        self.lab_rows = round_up((self.cap + self.groups - 1) // self.groups, 8)
        self.rows = self.half + self.lab_rows
        self.slots = BLK_DEV * LANES
        self.per_tile = LANES // self.lab_rows
        self.lab_tiles = (peers + self.per_tile - 1) // self.per_tile
        assert 2 * fields == LANES


def pack_kernel(plan, rec_hbm, mass_hbm, forest_hbm, block_hbm, slot_hbm, out_ref,
                rec_ref, mass_ref, forest_ref, block_ref, slot_ref,
                rows_in, rows_out, packed, flat, members, target, target_s, sem, in_sems,
                out_sems):
    snaps, fields, peers, tiles = plan.snaps, plan.fields, plan.peers, plan.tiles
    loads = []
    for index, (source, held) in enumerate((
            (block_hbm, block_ref), (slot_hbm, slot_ref), (forest_hbm, forest_ref),
            (mass_hbm, mass_ref), (rec_hbm, rec_ref))):
        load = pltpu.make_async_copy(source, held, in_sems.at[index])
        load.start()
        loads.append(load)
    lane = lax.broadcasted_iota(jnp.int32, (8, LANES), 1)
    for load in loads[:4]:
        load.wait()
    for chunk in range(plan.chunks):
        here = pl.ds(chunk * snaps, snaps)
        cut = pl.ds(chunk * LANES, LANES)
        flat[0, here, :] = block_ref[:, cut].astype(jnp.float32)
        flat[1, here, :] = slot_ref[:, cut].astype(jnp.float32)
        flat[2, here, :] = forest_ref[:, cut].astype(jnp.float32)
        flat[3, here, :] = mass_ref[:, cut]
    block = flat[0]
    mass = flat[3]
    for owner in range(peers):
        inside = (block >= owner * BLK_DEV) & (block < (owner + 1) * BLK_DEV)
        members[pl.ds(owner * tiles, tiles), :] = jnp.where(inside, 1.0, 0.0).astype(jnp.bfloat16)
    down = lax.broadcasted_iota(jnp.int32, (LANES, LANES), 0)
    across = lax.broadcasted_iota(jnp.int32, (LANES, LANES), 1)
    upper = jnp.where(down < across, 1.0, 0.0).astype(jnp.bfloat16)
    every = jnp.ones((LANES, LANES), jnp.bfloat16)
    lower = jnp.where(
        lax.broadcasted_iota(jnp.int32, (tiles, tiles), 0)
        > lax.broadcasted_iota(jnp.int32, (tiles, tiles), 1), 1.0, 0.0).astype(jnp.bfloat16)
    place = jnp.zeros((tiles, LANES), jnp.float32)
    owner_of = jnp.zeros((tiles, LANES), jnp.float32)
    for owner in range(peers):
        member = members[pl.ds(owner * tiles, tiles), :]
        within = jnp.dot(member, upper, preferred_element_type=jnp.float32)
        totals = jnp.dot(member, every, preferred_element_type=jnp.float32).astype(jnp.bfloat16)
        before = jnp.dot(lower, totals, preferred_element_type=jnp.float32)
        chosen = member.astype(jnp.float32)
        place = place + chosen * (within + before + float(owner * plan.cap))
        owner_of = owner_of + chosen * float(owner)
    target[...] = place.astype(jnp.int32)
    copy = pltpu.make_async_copy(target, target_s, sem)
    copy.start()
    flat[1] = (block - owner_of * float(BLK_DEV)) * float(LANES) + flat[1]
    flat[2] = flat[2] - owner_of * float(FOR_DEV)
    total = jnp.sum(mass)

    loads[4].wait()
    sub = lax.broadcasted_iota(jnp.int32, (8, LANES), 0)
    zeros = jnp.zeros((LANES - fields - 8, LANES), jnp.float32)
    for chunk in range(plan.chunks):
        for snap in range(snaps):
            row = chunk * snaps + snap
            values = rec_ref[:, snap, pl.ds(chunk * LANES, LANES)]
            label = jnp.where(sub == 0, flat[3, pl.ds(row, 1), :], total)
            label = jnp.where(sub == 1, flat[1, pl.ds(row, 1), :], label)
            label = jnp.where(sub == 2, flat[2, pl.ds(row, 1), :], label)
            whole = jnp.concatenate([values, label, zeros], axis=0)
            rows_in[pl.ds(row * LANES, LANES), :] = whole.T

    empty = jnp.where(lane == fields + 1, float(plan.slots),
                      jnp.where(lane == fields + 3, total, 0.0))

    def clear(step, carry):
        for part in range(8):
            rows_out[pl.ds(pl.multiple_of(step * 64 + part * 8, 8), 8), :] = empty
        return carry

    lax.fori_loop(0, peers * plan.cap // 64, clear, 0)
    copy.wait()

    def scatter(row, carry):
        for col in range(LANES):
            to = target_s[row, col]
            rows_out[pl.ds(to, 1), :] = rows_in[pl.ds(row * LANES + col, 1), :]
        return carry

    lax.fori_loop(0, tiles, scatter, 0)

    def squeeze(peer, carry):
        start = peer * plan.cap
        for step in range(plan.half // 8):
            low = rows_out[pl.ds(pl.multiple_of(start + step * 8, 8), 8), :]
            high = rows_out[pl.ds(pl.multiple_of(start + plan.half + step * 8, 8), 8), :]
            packed[peer, pl.ds(step * 8, 8), :] = jnp.where(
                lane < fields, low, pltpu.roll(high, fields, 1))
        per = plan.lab_rows // 8
        for part in range(per):
            gathered = jnp.zeros((8, LANES), jnp.float32)
            for group in range(plan.groups):
                tile = group * per + part
                if tile * 8 < plan.cap:
                    piece = rows_out[pl.ds(pl.multiple_of(start + tile * 8, 8), 8), :]
                    moved = pltpu.roll(piece, (group * LABELS - fields) % LANES, 1)
                    gathered = jnp.where(lane // LABELS == group, moved, gathered)
            packed[peer, pl.ds(plan.half + part * 8, 8), :] = gathered
        pltpu.make_async_copy(packed.at[peer], out_ref.at[peer], out_sems.at[peer]).start()
        return carry

    lax.fori_loop(0, peers, squeeze, 0)
    for peer in range(peers):
        pltpu.make_async_copy(packed.at[peer], out_ref.at[peer], out_sems.at[peer]).wait()


def partner(me, step, peers):
    if peers & (peers - 1):
        return lax.rem(me + step, peers)
    other, bit = jnp.int32(0), 1
    while bit < peers:
        mine = lax.rem(lax.div(me, jnp.int32(bit)), jnp.int32(2))
        other = other + bit * (1 - mine if step & bit else mine)
        bit *= 2
    return other


def exchange_kernel(plan, n_ha, send_ref, arrived_ref, labels_ref, got_ref,
                    send_sem, recv_sem, own_sem):
    fields, peers = plan.fields, plan.peers
    me = lax.axis_index("sa") * n_ha + lax.axis_index("ha")
    barrier = pltpu.get_barrier_semaphore()

    def where_is(peer):
        return {"sa": lax.div(peer, jnp.int32(n_ha)), "ha": lax.rem(peer, jnp.int32(n_ha))}

    others = [partner(me, step, peers) for step in range(1, peers)]
    for peer in others:
        pl.semaphore_signal(barrier, inc=1, device_id=where_is(peer),
                            device_id_type=pl.DeviceIdType.MESH)
    pl.semaphore_wait(barrier, peers - 1)
    copies = []
    for step, peer in enumerate(others, 1):
        copy = pltpu.make_async_remote_copy(
            src_ref=send_ref.at[peer],
            dst_ref=got_ref.at[step],
            send_sem=send_sem.at[step],
            recv_sem=recv_sem.at[step],
            device_id=where_is(peer),
            device_id_type=pl.DeviceIdType.MESH,
        )
        copy.start()
        copies.append(copy)
    own = pltpu.make_async_copy(send_ref.at[me], got_ref.at[0], own_sem)
    own.start()
    own.wait()

    per = plan.lab_rows // 8
    lane = lax.broadcasted_iota(jnp.int32, (8, LANES), 1)
    in_labels = (lane >= fields) & (lane < fields + LABELS)

    def spread(step):
        start = step * plan.cap
        for tile in range(plan.cap // 8):
            side, at = tile // (plan.half // 8), tile % (plan.half // 8)
            record = got_ref[step, pl.ds(at * 8, 8), :]
            group, part = tile // per, tile % per
            label = got_ref[step, pl.ds(plan.half + part * 8, 8), :]
            label = pltpu.roll(label, (fields - group * LABELS) % LANES, 1)
            if side:
                record = pltpu.roll(record, fields, 1)
            arrived_ref[pl.ds(pl.multiple_of(start + tile * 8, 8), 8), :] = jnp.where(
                lane < fields, record, jnp.where(in_labels, label, 0.0))

    spread(0)
    peer_of = others[0]

    def arrive(step, carry):
        pltpu.make_async_remote_copy(
            src_ref=send_ref.at[0], dst_ref=got_ref.at[step],
            send_sem=send_sem.at[step], recv_sem=recv_sem.at[step],
            device_id=where_is(peer_of), device_id_type=pl.DeviceIdType.MESH,
        ).wait_recv()
        spread(step)
        return carry

    lax.fori_loop(1, peers, arrive, 0)
    for tile in range(plan.lab_tiles):
        first = tile * plan.per_tile
        count = min(plan.per_tile, peers - first)
        pieces = [got_ref[first + k, pl.ds(plan.half, plan.lab_rows), :] for k in range(count)]
        rest = LANES - count * plan.lab_rows
        if rest:
            pieces.append(jnp.zeros((rest, LANES), jnp.float32))
        labels_ref[tile] = jnp.concatenate(pieces, axis=0).T.astype(jnp.int32)
    for copy in copies:
        copy.wait_send()


def unpack_kernel(plan, arrived, labels, blocks_ref, mass_ref, fmass_ref, mean_ref,
                  second_ref, placed, member_s, value_s, labels_s, sem):
    fields, peers = plan.fields, plan.peers
    copy = pltpu.make_async_copy(labels, labels_s, sem)
    copy.start()

    def clear(step, carry):
        for part in range(8):
            placed[pl.ds(pl.multiple_of(step * 64 + part * 8, 8), 8), :] = jnp.zeros(
                (8, LANES), jnp.float32)
        return carry

    lax.fori_loop(0, plan.slots // 64, clear, 0)
    copy.wait()

    for peer in range(peers):
        tile, offset = peer // plan.per_tile, peer % plan.per_tile * plan.lab_rows
        whole = plan.cap // plan.lab_rows

        def scatter(group, carry, rows=plan.lab_rows, peer=peer, tile=tile, offset=offset):
            for row in range(rows):
                to = labels_s[tile, group * LABELS + 1, offset + row]
                placed[pl.ds(to, 1), :] = arrived[
                    pl.ds(peer * plan.cap + group * plan.lab_rows + row, 1), :]
            return carry

        lax.fori_loop(0, whole, scatter, 0)
        if plan.cap % plan.lab_rows:
            scatter(whole, 0, rows=plan.cap % plan.lab_rows)

    total = jnp.zeros((1, 1), jnp.float32)
    for peer in range(peers):
        total = total + arrived[pl.ds(peer * plan.cap, 1), :][:, fields + 3:fields + 4]
    forests = lax.broadcasted_iota(jnp.int32, (FOR_DEV, LANES), 0).astype(jnp.float32)
    wide = lax.broadcasted_iota(jnp.int32, (LANES, LANES), 1)

    weights = jnp.zeros((FOR_DEV, LANES), jnp.float32)
    span = 4

    def some_blocks(part, weights):
        for inner in range(span):
            block = part * span + inner
            rows = placed[pl.ds(pl.multiple_of(block * LANES, LANES), LANES), :]
            turned = rows.T
            blocks_ref[pl.ds(block, fields, stride=BLK_DEV), :] = turned[:fields]
            mass_row = turned[fields:fields + 1]
            mass_ref[pl.ds(block, 1), :] = mass_row
            hit = turned[fields + 2:fields + 3] == forests
            weights = weights + jnp.where(hit, mass_row, 0.0)
            member_s[part, :, inner * LANES:(inner + 1) * LANES] = jnp.where(
                hit, 1.0, 0.0).astype(jnp.bfloat16)
            mass = rows[:, fields:fields + 1]
            value = jnp.where(wide < fields, rows, pltpu.roll(rows, fields, 1))
            scaled = mass * value
            scaled = jnp.where(wide < fields, scaled, scaled * value)
            high = scaled.astype(jnp.bfloat16)
            low = (scaled - high.astype(jnp.float32)).astype(jnp.bfloat16)
            here = pl.ds(inner * LANES, LANES)
            value_s[part, here, :LANES] = high
            value_s[part, here, LANES:] = low
        return weights

    weights = lax.fori_loop(0, BLK_DEV // span, some_blocks, weights)
    sums = jnp.zeros((FOR_DEV, 2 * LANES), jnp.float32)
    for part in range(BLK_DEV // span):
        sums = sums + jnp.dot(member_s[part], value_s[part], preferred_element_type=jnp.float32)
    sums = sums[:, :LANES] + sums[:, LANES:]
    weight = jnp.sum(weights.T, axis=0, keepdims=True)
    sums = sums.T
    fmass_ref[...] = weight * (float(FOR_DEV * peers) / total)
    mean_ref[...] = sums[:fields] / weight
    second_ref[...] = sums[fields:] / weight


def on_device(n_ha, peers, records, halo_mass, forest_id, dest_block, dest_slot):
    fields, snaps, halos = records.shape
    plan = Plan(fields, snaps, halos, peers)
    f32, i32 = jnp.float32, jnp.int32
    hbm = pl.BlockSpec(memory_space=pltpu.HBM)
    vmem = pl.BlockSpec(memory_space=pltpu.VMEM)
    full = pltpu.CompilerParams(vmem_limit_bytes=67043328)
    big = pltpu.CompilerParams(vmem_limit_bytes=48 * 1024 * 1024)
    send = pl.pallas_call(
        functools.partial(pack_kernel, plan),
        out_shape=jax.ShapeDtypeStruct((peers, plan.rows, LANES), f32),
        in_specs=[hbm] * 5,
        out_specs=hbm,
        scratch_shapes=[
            pltpu.VMEM(records.shape, f32),
            pltpu.VMEM((snaps, halos), f32),
            pltpu.VMEM((snaps, halos), i32),
            pltpu.VMEM((snaps, halos), i32),
            pltpu.VMEM((snaps, halos), i32),
            pltpu.VMEM((plan.local, LANES), f32),
            pltpu.VMEM((peers * plan.cap, LANES), f32),
            pltpu.VMEM((peers, plan.rows, LANES), f32),
            pltpu.VMEM((4, plan.tiles, LANES), f32),
            pltpu.VMEM((peers * plan.tiles, LANES), jnp.bfloat16),
            pltpu.VMEM((plan.tiles, LANES), i32),
            pltpu.SMEM((plan.tiles, LANES), i32),
            pltpu.SemaphoreType.DMA,
            pltpu.SemaphoreType.DMA((5,)),
            pltpu.SemaphoreType.DMA((peers,)),
        ],
        compiler_params=full,
        name="pack",
    )(records, halo_mass, forest_id, dest_block, dest_slot)
    kept = (peers * plan.cap + plan.lab_tiles * LANES + 1024) * LANES * 4
    arrived, labels = pl.pallas_call(
        functools.partial(exchange_kernel, plan, n_ha),
        out_shape=(
            jax.ShapeDtypeStruct((peers * plan.cap, LANES), f32),
            jax.ShapeDtypeStruct((plan.lab_tiles, LANES, LANES), i32),
        ),
        in_specs=[hbm],
        out_specs=(vmem, vmem),
        scratch_shapes=[
            pltpu.VMEM(send.shape, f32),
            pltpu.SemaphoreType.DMA((peers,)),
            pltpu.SemaphoreType.DMA((peers,)),
            pltpu.SemaphoreType.DMA,
        ],
        compiler_params=pltpu.CompilerParams(
            collective_id=0, has_side_effects=True, vmem_limit_bytes=67043328 - kept),
        name="exchange",
    )(send)
    blocks, block_mass, forest_mass, mean, second = pl.pallas_call(
        functools.partial(unpack_kernel, plan),
        out_shape=(
            jax.ShapeDtypeStruct((fields * BLK_DEV, LANES), f32),
            jax.ShapeDtypeStruct((BLK_DEV, LANES), f32),
            jax.ShapeDtypeStruct((1, FOR_DEV), f32),
            jax.ShapeDtypeStruct((fields, FOR_DEV), f32),
            jax.ShapeDtypeStruct((fields, FOR_DEV), f32),
        ),
        in_specs=[vmem, vmem],
        out_specs=(vmem,) * 5,
        scratch_shapes=[
            pltpu.VMEM((plan.slots + 8, LANES), f32),
            pltpu.VMEM((10, FOR_DEV, 4 * LANES), jnp.bfloat16),
            pltpu.VMEM((10, 4 * LANES, 2 * LANES), jnp.bfloat16),
            pltpu.SMEM((plan.lab_tiles, LANES, LANES), i32),
            pltpu.SemaphoreType.DMA,
        ],
        compiler_params=big,
        name="unpack",
    )(arrived, labels)
    return (
        blocks.reshape(fields, BLK_DEV, LANES),
        block_mass,
        forest_mass.reshape(FOR_DEV),
        mean,
        second,
    )


def solution(mesh):
    n_ha = mesh.shape["ha"]
    peers = mesh.shape["sa"] * n_ha
    in_specs = (
        P(None, "sa", ("row", "ha")),
        P("sa", ("row", "ha")),
        P("sa", ("row", "ha")),
        P("sa", ("row", "ha")),
        P("sa", ("row", "ha")),
    )
    out_specs = (
        P(None, ("row", "sa", "ha"), None),
        P(("row", "sa", "ha"), None),
        P(("row", "sa", "ha")),
        P(None, ("row", "sa", "ha")),
        P(None, ("row", "sa", "ha")),
    )
    return jax.shard_map(
        functools.partial(on_device, n_ha, peers),
        mesh=mesh, in_specs=in_specs, out_specs=out_specs, check_vma=False
    )
```

```python
import functools

import jax
import jax.numpy as jnp
from jax import lax
from jax.experimental import pallas as pl
from jax.experimental.pallas import tpu as pltpu
from jax.sharding import PartitionSpec as P

FOR_DEV = 128
BLK_DEV = 40
LANES = 128
LABELS = 4


def round_up(value, unit):
    return (value + unit - 1) // unit * unit


class Plan:
    def __init__(self, fields, snaps, halos, peers):
        self.fields, self.snaps, self.halos, self.peers = fields, snaps, halos, peers
        self.local = snaps * halos
        self.tiles = self.local // LANES
        self.chunks = halos // LANES
        capacity = 11 * (self.local // peers) // 8
        self.cap = round_up(capacity, 16)
        self.half = self.cap // 2
        self.groups = LANES // LABELS
        self.lab_rows = round_up((self.cap + self.groups - 1) // self.groups, 8)
        self.rows = self.half + self.lab_rows
        self.slots = BLK_DEV * LANES
        self.per_tile = LANES // self.lab_rows
        self.lab_tiles = (peers + self.per_tile - 1) // self.per_tile
        assert 2 * fields == LANES


def pack_kernel(plan, rec_hbm, mass_hbm, forest_hbm, block_hbm, slot_hbm, out_ref,
                rec_ref, mass_ref, forest_ref, block_ref, slot_ref,
                rows_in, rows_out, packed, flat, members, target, target_s, sem, in_sems,
                out_sems):
    snaps, fields, peers, tiles = plan.snaps, plan.fields, plan.peers, plan.tiles
    loads = []
    for index, (source, held) in enumerate((
            (block_hbm, block_ref), (slot_hbm, slot_ref), (forest_hbm, forest_ref),
            (mass_hbm, mass_ref), (rec_hbm, rec_ref))):
        load = pltpu.make_async_copy(source, held, in_sems.at[index])
        load.start()
        loads.append(load)
    lane = lax.broadcasted_iota(jnp.int32, (8, LANES), 1)
    for load in loads[:4]:
        load.wait()
    for chunk in range(plan.chunks):
        here = pl.ds(chunk * snaps, snaps)
        cut = pl.ds(chunk * LANES, LANES)
        flat[0, here, :] = block_ref[:, cut].astype(jnp.float32)
        flat[1, here, :] = slot_ref[:, cut].astype(jnp.float32)
        flat[2, here, :] = forest_ref[:, cut].astype(jnp.float32)
        flat[3, here, :] = mass_ref[:, cut]
    block = flat[0]
    mass = flat[3]
    for owner in range(peers):
        inside = (block >= owner * BLK_DEV) & (block < (owner + 1) * BLK_DEV)
        members[pl.ds(owner * tiles, tiles), :] = jnp.where(inside, 1.0, 0.0).astype(jnp.bfloat16)
    down = lax.broadcasted_iota(jnp.int32, (LANES, LANES), 0)
    across = lax.broadcasted_iota(jnp.int32, (LANES, LANES), 1)
    upper = jnp.where(down < across, 1.0, 0.0).astype(jnp.bfloat16)
    every = jnp.ones((LANES, LANES), jnp.bfloat16)
    lower = jnp.where(
        lax.broadcasted_iota(jnp.int32, (tiles, tiles), 0)
        > lax.broadcasted_iota(jnp.int32, (tiles, tiles), 1), 1.0, 0.0).astype(jnp.bfloat16)
    place = jnp.zeros((tiles, LANES), jnp.float32)
    owner_of = jnp.zeros((tiles, LANES), jnp.float32)
    for owner in range(peers):
        member = members[pl.ds(owner * tiles, tiles), :]
        within = jnp.dot(member, upper, preferred_element_type=jnp.float32)
        totals = jnp.dot(member, every, preferred_element_type=jnp.float32).astype(jnp.bfloat16)
        before = jnp.dot(lower, totals, preferred_element_type=jnp.float32)
        chosen = member.astype(jnp.float32)
        place = place + chosen * (within + before + float(owner * plan.cap))
        owner_of = owner_of + chosen * float(owner)
    target[...] = place.astype(jnp.int32)
    copy = pltpu.make_async_copy(target, target_s, sem)
    copy.start()
    flat[1] = (block - owner_of * float(BLK_DEV)) * float(LANES) + flat[1]
    flat[2] = flat[2] - owner_of * float(FOR_DEV)
    total = jnp.sum(mass)

    loads[4].wait()
    sub = lax.broadcasted_iota(jnp.int32, (8, LANES), 0)
    zeros = jnp.zeros((LANES - fields - 8, LANES), jnp.float32)
    for chunk in range(plan.chunks):
        for snap in range(snaps):
            row = chunk * snaps + snap
            values = rec_ref[:, snap, pl.ds(chunk * LANES, LANES)]
            label = jnp.where(sub == 0, flat[3, pl.ds(row, 1), :], total)
            label = jnp.where(sub == 1, flat[1, pl.ds(row, 1), :], label)
            label = jnp.where(sub == 2, flat[2, pl.ds(row, 1), :], label)
            whole = jnp.concatenate([values, label, zeros], axis=0)
            rows_in[pl.ds(row * LANES, LANES), :] = whole.T

    empty = jnp.where(lane == fields + 1, float(plan.slots),
                      jnp.where(lane == fields + 3, total, 0.0))

    def clear(step, carry):
        for part in range(8):
            rows_out[pl.ds(pl.multiple_of(step * 64 + part * 8, 8), 8), :] = empty
        return carry

    lax.fori_loop(0, peers * plan.cap // 64, clear, 0)
    copy.wait()

    def scatter(row, carry):
        for col in range(LANES):
            to = target_s[row, col]
            rows_out[pl.ds(to, 1), :] = rows_in[pl.ds(row * LANES + col, 1), :]
        return carry

    lax.fori_loop(0, tiles, scatter, 0)

    def squeeze(peer, carry):
        start = peer * plan.cap
        for step in range(plan.half // 8):
            low = rows_out[pl.ds(pl.multiple_of(start + step * 8, 8), 8), :]
            high = rows_out[pl.ds(pl.multiple_of(start + plan.half + step * 8, 8), 8), :]
            packed[peer, pl.ds(step * 8, 8), :] = jnp.where(
                lane < fields, low, pltpu.roll(high, fields, 1))
        per = plan.lab_rows // 8
        for part in range(per):
            gathered = jnp.zeros((8, LANES), jnp.float32)
            for group in range(plan.groups):
                tile = group * per + part
                if tile * 8 < plan.cap:
                    piece = rows_out[pl.ds(pl.multiple_of(start + tile * 8, 8), 8), :]
                    moved = pltpu.roll(piece, (group * LABELS - fields) % LANES, 1)
                    gathered = jnp.where(lane // LABELS == group, moved, gathered)
            packed[peer, pl.ds(plan.half + part * 8, 8), :] = gathered
        pltpu.make_async_copy(packed.at[peer], out_ref.at[peer], out_sems.at[peer]).start()
        return carry

    lax.fori_loop(0, peers, squeeze, 0)
    for peer in range(peers):
        pltpu.make_async_copy(packed.at[peer], out_ref.at[peer], out_sems.at[peer]).wait()


def partner(me, step, peers):
    if peers & (peers - 1):
        return lax.rem(me + step, peers)
    other, bit = jnp.int32(0), 1
    while bit < peers:
        mine = lax.rem(lax.div(me, jnp.int32(bit)), jnp.int32(2))
        other = other + bit * (1 - mine if step & bit else mine)
        bit *= 2
    return other


def exchange_kernel(plan, n_ha, send_ref, arrived_hbm, labels_hbm, got_ref, arrived_ref,
                    labels_ref, send_sem, recv_sem, own_sem, out_sems):
    fields, peers = plan.fields, plan.peers
    me = lax.axis_index("sa") * n_ha + lax.axis_index("ha")
    barrier = pltpu.get_barrier_semaphore()

    def where_is(peer):
        return {"sa": lax.div(peer, jnp.int32(n_ha)), "ha": lax.rem(peer, jnp.int32(n_ha))}

    others = [partner(me, step, peers) for step in range(1, peers)]
    for peer in others:
        pl.semaphore_signal(barrier, inc=1, device_id=where_is(peer),
                            device_id_type=pl.DeviceIdType.MESH)
    pl.semaphore_wait(barrier, peers - 1)
    copies = []
    for step, peer in enumerate(others, 1):
        copy = pltpu.make_async_remote_copy(
            src_ref=send_ref.at[peer],
            dst_ref=got_ref.at[step],
            send_sem=send_sem.at[step],
            recv_sem=recv_sem.at[step],
            device_id=where_is(peer),
            device_id_type=pl.DeviceIdType.MESH,
        )
        copy.start()
        copies.append(copy)
    own = pltpu.make_async_copy(send_ref.at[me], got_ref.at[0], own_sem)
    own.start()
    own.wait()

    per = plan.lab_rows // 8
    lane = lax.broadcasted_iota(jnp.int32, (8, LANES), 1)
    in_labels = (lane >= fields) & (lane < fields + LABELS)

    def spread(step):
        start = step * plan.cap
        for tile in range(plan.cap // 8):
            side, at = tile // (plan.half // 8), tile % (plan.half // 8)
            record = got_ref[step, pl.ds(at * 8, 8), :]
            group, part = tile // per, tile % per
            label = got_ref[step, pl.ds(plan.half + part * 8, 8), :]
            label = pltpu.roll(label, (fields - group * LABELS) % LANES, 1)
            if side:
                record = pltpu.roll(record, fields, 1)
            arrived_ref[pl.ds(pl.multiple_of(start + tile * 8, 8), 8), :] = jnp.where(
                lane < fields, record, jnp.where(in_labels, label, 0.0))
        put(step).start()

    def put(step):
        here = pl.ds(pl.multiple_of(step * plan.cap, 8), plan.cap)
        return pltpu.make_async_copy(
            arrived_ref.at[here, :], arrived_hbm.at[here, :], out_sems.at[step])

    spread(0)
    peer_of = others[0]

    def arrive(step, carry):
        pltpu.make_async_remote_copy(
            src_ref=send_ref.at[0], dst_ref=got_ref.at[step],
            send_sem=send_sem.at[step], recv_sem=recv_sem.at[step],
            device_id=where_is(peer_of), device_id_type=pl.DeviceIdType.MESH,
        ).wait_recv()
        spread(step)
        return carry

    lax.fori_loop(1, peers, arrive, 0)
    for tile in range(plan.lab_tiles):
        first = tile * plan.per_tile
        count = min(plan.per_tile, peers - first)
        pieces = [got_ref[first + k, pl.ds(plan.half, plan.lab_rows), :] for k in range(count)]
        rest = LANES - count * plan.lab_rows
        if rest:
            pieces.append(jnp.zeros((rest, LANES), jnp.float32))
        labels_ref[tile] = jnp.concatenate(pieces, axis=0).T.astype(jnp.int32)
    put_labels = pltpu.make_async_copy(labels_ref, labels_hbm, out_sems.at[peers])
    put_labels.start()
    for copy in copies:
        copy.wait_send()
    for step in range(peers):
        put(step).wait()
    put_labels.wait()


def unpack_kernel(plan, arrived_hbm, labels, blocks_ref, mass_ref, fmass_ref, mean_ref,
                  second_ref, arrived, placed, member_s, value_s, labels_s, sem, in_sems):
    fields, peers = plan.fields, plan.peers

    def take(step):
        here = pl.ds(pl.multiple_of(step * plan.cap, 8), plan.cap)
        return pltpu.make_async_copy(
            arrived_hbm.at[here, :], arrived.at[here, :], in_sems.at[step])

    copy = pltpu.make_async_copy(labels, labels_s, sem)
    copy.start()
    for step in range(peers):
        take(step).start()

    def clear(step, carry):
        for part in range(8):
            placed[pl.ds(pl.multiple_of(step * 64 + part * 8, 8), 8), :] = jnp.zeros(
                (8, LANES), jnp.float32)
        return carry

    lax.fori_loop(0, plan.slots // 64, clear, 0)
    copy.wait()

    def scatter(peer, carry):
        tile = lax.div(peer, jnp.int32(plan.per_tile))
        offset = lax.rem(peer, jnp.int32(plan.per_tile)) * plan.lab_rows
        start = peer * plan.cap
        take(peer).wait()
        for rank in range(plan.cap):
            group, row = rank // plan.lab_rows, rank % plan.lab_rows
            to = labels_s[tile, group * LABELS + 1, offset + row]
            placed[pl.ds(to, 1), :] = arrived[pl.ds(start + rank, 1), :]
        return carry

    lax.fori_loop(0, peers, scatter, 0)

    total = jnp.zeros((1, 1), jnp.float32)
    for peer in range(peers):
        total = total + arrived[pl.ds(peer * plan.cap, 1), :][:, fields + 3:fields + 4]
    forests = lax.broadcasted_iota(jnp.int32, (FOR_DEV, LANES), 0).astype(jnp.float32)
    wide = lax.broadcasted_iota(jnp.int32, (LANES, LANES), 1)

    weights = jnp.zeros((FOR_DEV, LANES), jnp.float32)
    span = 4

    def some_blocks(part, weights):
        for inner in range(span):
            block = part * span + inner
            rows = placed[pl.ds(pl.multiple_of(block * LANES, LANES), LANES), :]
            turned = rows.T
            blocks_ref[pl.ds(block, fields, stride=BLK_DEV), :] = turned[:fields]
            mass_row = turned[fields:fields + 1]
            mass_ref[pl.ds(block, 1), :] = mass_row
            hit = turned[fields + 2:fields + 3] == forests
            weights = weights + jnp.where(hit, mass_row, 0.0)
            member_s[part, :, inner * LANES:(inner + 1) * LANES] = jnp.where(
                hit, 1.0, 0.0).astype(jnp.bfloat16)
            mass = rows[:, fields:fields + 1]
            value = jnp.where(wide < fields, rows, pltpu.roll(rows, fields, 1))
            scaled = mass * value
            scaled = jnp.where(wide < fields, scaled, scaled * value)
            high = scaled.astype(jnp.bfloat16)
            low = (scaled - high.astype(jnp.float32)).astype(jnp.bfloat16)
            here = pl.ds(inner * LANES, LANES)
            value_s[part, here, :LANES] = high
            value_s[part, here, LANES:] = low
        return weights

    weights = lax.fori_loop(0, BLK_DEV // span, some_blocks, weights)
    sums = jnp.zeros((FOR_DEV, 2 * LANES), jnp.float32)
    for part in range(BLK_DEV // span):
        sums = sums + jnp.dot(member_s[part], value_s[part], preferred_element_type=jnp.float32)
    sums = sums[:, :LANES] + sums[:, LANES:]
    weight = jnp.sum(weights.T, axis=0, keepdims=True)
    sums = sums.T
    fmass_ref[...] = weight * (float(FOR_DEV * peers) / total)
    mean_ref[...] = sums[:fields] / weight
    second_ref[...] = sums[fields:] / weight


def on_device(n_ha, peers, records, halo_mass, forest_id, dest_block, dest_slot):
    fields, snaps, halos = records.shape
    plan = Plan(fields, snaps, halos, peers)
    f32, i32 = jnp.float32, jnp.int32
    hbm = pl.BlockSpec(memory_space=pltpu.HBM)
    vmem = pl.BlockSpec(memory_space=pltpu.VMEM)
    full = pltpu.CompilerParams(vmem_limit_bytes=67043328)
    send = pl.pallas_call(
        functools.partial(pack_kernel, plan),
        out_shape=jax.ShapeDtypeStruct((peers, plan.rows, LANES), f32),
        in_specs=[hbm] * 5,
        out_specs=hbm,
        scratch_shapes=[
            pltpu.VMEM(records.shape, f32),
            pltpu.VMEM((snaps, halos), f32),
            pltpu.VMEM((snaps, halos), i32),
            pltpu.VMEM((snaps, halos), i32),
            pltpu.VMEM((snaps, halos), i32),
            pltpu.VMEM((plan.local, LANES), f32),
            pltpu.VMEM((peers * plan.cap, LANES), f32),
            pltpu.VMEM((peers, plan.rows, LANES), f32),
            pltpu.VMEM((4, plan.tiles, LANES), f32),
            pltpu.VMEM((peers * plan.tiles, LANES), jnp.bfloat16),
            pltpu.VMEM((plan.tiles, LANES), i32),
            pltpu.SMEM((plan.tiles, LANES), i32),
            pltpu.SemaphoreType.DMA,
            pltpu.SemaphoreType.DMA((5,)),
            pltpu.SemaphoreType.DMA((peers,)),
        ],
        compiler_params=full,
        name="pack",
    )(records, halo_mass, forest_id, dest_block, dest_slot)
    arrived, labels = pl.pallas_call(
        functools.partial(exchange_kernel, plan, n_ha),
        out_shape=(
            jax.ShapeDtypeStruct((peers * plan.cap, LANES), f32),
            jax.ShapeDtypeStruct((plan.lab_tiles, LANES, LANES), i32),
        ),
        in_specs=[hbm],
        out_specs=(hbm, hbm),
        scratch_shapes=[
            pltpu.VMEM(send.shape, f32),
            pltpu.VMEM((peers * plan.cap, LANES), f32),
            pltpu.VMEM((plan.lab_tiles, LANES, LANES), i32),
            pltpu.SemaphoreType.DMA((peers,)),
            pltpu.SemaphoreType.DMA((peers,)),
            pltpu.SemaphoreType.DMA,
            pltpu.SemaphoreType.DMA((peers + 1,)),
        ],
        compiler_params=pltpu.CompilerParams(
            collective_id=0, has_side_effects=True, vmem_limit_bytes=67043328),
        name="exchange",
    )(send)
    blocks, block_mass, forest_mass, mean, second = pl.pallas_call(
        functools.partial(unpack_kernel, plan),
        out_shape=(
            jax.ShapeDtypeStruct((fields * BLK_DEV, LANES), f32),
            jax.ShapeDtypeStruct((BLK_DEV, LANES), f32),
            jax.ShapeDtypeStruct((1, FOR_DEV), f32),
            jax.ShapeDtypeStruct((fields, FOR_DEV), f32),
            jax.ShapeDtypeStruct((fields, FOR_DEV), f32),
        ),
        in_specs=[hbm, hbm],
        out_specs=(vmem,) * 5,
        scratch_shapes=[
            pltpu.VMEM((peers * plan.cap, LANES), f32),
            pltpu.VMEM((plan.slots + 8, LANES), f32),
            pltpu.VMEM((10, FOR_DEV, 4 * LANES), jnp.bfloat16),
            pltpu.VMEM((10, 4 * LANES, 2 * LANES), jnp.bfloat16),
            pltpu.SMEM((plan.lab_tiles, LANES, LANES), i32),
            pltpu.SemaphoreType.DMA,
            pltpu.SemaphoreType.DMA((peers,)),
        ],
        compiler_params=full,
        name="unpack",
    )(arrived, labels)
    return (
        blocks.reshape(fields, BLK_DEV, LANES),
        block_mass,
        forest_mass.reshape(FOR_DEV),
        mean,
        second,
    )


def solution(mesh):
    n_ha = mesh.shape["ha"]
    peers = mesh.shape["sa"] * n_ha
    in_specs = (
        P(None, "sa", ("row", "ha")),
        P("sa", ("row", "ha")),
        P("sa", ("row", "ha")),
        P("sa", ("row", "ha")),
        P("sa", ("row", "ha")),
    )
    out_specs = (
        P(None, ("row", "sa", "ha"), None),
        P(("row", "sa", "ha"), None),
        P(("row", "sa", "ha")),
        P(None, ("row", "sa", "ha")),
        P(None, ("row", "sa", "ha")),
    )
    return jax.shard_map(
        functools.partial(on_device, n_ha, peers),
        mesh=mesh, in_specs=in_specs, out_specs=out_specs, check_vma=False
    )
```

```python
import functools

import jax
import jax.numpy as jnp
from jax import lax
from jax.experimental import pallas as pl
from jax.experimental.pallas import tpu as pltpu
from jax.sharding import PartitionSpec as P

FOR_DEV = 128
BLK_DEV = 40
LANES = 128
LABELS = 4


def round_up(value, unit):
    return (value + unit - 1) // unit * unit


class Plan:
    def __init__(self, fields, snaps, halos, peers):
        self.fields, self.snaps, self.halos, self.peers = fields, snaps, halos, peers
        self.local = snaps * halos
        self.tiles = self.local // LANES
        self.chunks = halos // LANES
        capacity = 11 * (self.local // peers) // 8
        self.cap = round_up(capacity, 16)
        self.half = self.cap // 2
        self.groups = LANES // LABELS
        self.lab_rows = round_up((self.cap + self.groups - 1) // self.groups, 8)
        self.rows = self.half + self.lab_rows
        self.slots = BLK_DEV * LANES
        self.per_tile = LANES // self.lab_rows
        self.lab_tiles = (peers + self.per_tile - 1) // self.per_tile
        assert 2 * fields == LANES


def pack_kernel(plan, rec_hbm, mass_hbm, forest_hbm, block_hbm, slot_hbm, out_ref,
                rec_ref, mass_ref, forest_ref, block_ref, slot_ref,
                rows_in, rows_out, packed, flat, members, target, target_s, sem, in_sems,
                out_sems):
    snaps, fields, peers, tiles = plan.snaps, plan.fields, plan.peers, plan.tiles
    loads = []
    for index, (source, held) in enumerate((
            (block_hbm, block_ref), (slot_hbm, slot_ref), (forest_hbm, forest_ref),
            (mass_hbm, mass_ref), (rec_hbm, rec_ref))):
        load = pltpu.make_async_copy(source, held, in_sems.at[index])
        load.start()
        loads.append(load)
    lane = lax.broadcasted_iota(jnp.int32, (8, LANES), 1)
    for load in loads[:4]:
        load.wait()
    for chunk in range(plan.chunks):
        here = pl.ds(chunk * snaps, snaps)
        cut = pl.ds(chunk * LANES, LANES)
        flat[0, here, :] = block_ref[:, cut].astype(jnp.float32)
        flat[1, here, :] = slot_ref[:, cut].astype(jnp.float32)
        flat[2, here, :] = forest_ref[:, cut].astype(jnp.float32)
        flat[3, here, :] = mass_ref[:, cut]
    block = flat[0]
    mass = flat[3]
    for owner in range(peers):
        inside = (block >= owner * BLK_DEV) & (block < (owner + 1) * BLK_DEV)
        members[pl.ds(owner * tiles, tiles), :] = jnp.where(inside, 1.0, 0.0).astype(jnp.bfloat16)
    down = lax.broadcasted_iota(jnp.int32, (LANES, LANES), 0)
    across = lax.broadcasted_iota(jnp.int32, (LANES, LANES), 1)
    upper = jnp.where(down < across, 1.0, 0.0).astype(jnp.bfloat16)
    every = jnp.ones((LANES, LANES), jnp.bfloat16)
    lower = jnp.where(
        lax.broadcasted_iota(jnp.int32, (tiles, tiles), 0)
        > lax.broadcasted_iota(jnp.int32, (tiles, tiles), 1), 1.0, 0.0).astype(jnp.bfloat16)
    place = jnp.zeros((tiles, LANES), jnp.float32)
    owner_of = jnp.zeros((tiles, LANES), jnp.float32)
    for owner in range(peers):
        member = members[pl.ds(owner * tiles, tiles), :]
        within = jnp.dot(member, upper, preferred_element_type=jnp.float32)
        totals = jnp.dot(member, every, preferred_element_type=jnp.float32).astype(jnp.bfloat16)
        before = jnp.dot(lower, totals, preferred_element_type=jnp.float32)
        chosen = member.astype(jnp.float32)
        place = place + chosen * (within + before + float(owner * plan.cap))
        owner_of = owner_of + chosen * float(owner)
    target[...] = place.astype(jnp.int32)
    copy = pltpu.make_async_copy(target, target_s, sem)
    copy.start()
    flat[1] = (block - owner_of * float(BLK_DEV)) * float(LANES) + flat[1]
    flat[2] = flat[2] - owner_of * float(FOR_DEV)
    total = jnp.sum(mass)

    loads[4].wait()
    sub = lax.broadcasted_iota(jnp.int32, (8, LANES), 0)
    zeros = jnp.zeros((LANES - fields - 8, LANES), jnp.float32)
    for chunk in range(plan.chunks):
        for snap in range(snaps):
            row = chunk * snaps + snap
            values = rec_ref[:, snap, pl.ds(chunk * LANES, LANES)]
            label = jnp.where(sub == 0, flat[3, pl.ds(row, 1), :], total)
            label = jnp.where(sub == 1, flat[1, pl.ds(row, 1), :], label)
            label = jnp.where(sub == 2, flat[2, pl.ds(row, 1), :], label)
            whole = jnp.concatenate([values, label, zeros], axis=0)
            rows_in[pl.ds(row * LANES, LANES), :] = whole.T

    empty = jnp.where(lane == fields + 1, float(plan.slots),
                      jnp.where(lane == fields + 3, total, 0.0))

    def clear(step, carry):
        for part in range(8):
            rows_out[pl.ds(pl.multiple_of(step * 64 + part * 8, 8), 8), :] = empty
        return carry

    lax.fori_loop(0, peers * plan.cap // 64, clear, 0)
    copy.wait()

    def scatter(row, carry):
        for col in range(LANES):
            to = target_s[row, col]
            rows_out[pl.ds(to, 1), :] = rows_in[pl.ds(row * LANES + col, 1), :]
        return carry

    lax.fori_loop(0, tiles, scatter, 0)

    def squeeze(peer, carry):
        start = peer * plan.cap
        for step in range(plan.half // 8):
            low = rows_out[pl.ds(pl.multiple_of(start + step * 8, 8), 8), :]
            high = rows_out[pl.ds(pl.multiple_of(start + plan.half + step * 8, 8), 8), :]
            packed[peer, pl.ds(step * 8, 8), :] = jnp.where(
                lane < fields, low, pltpu.roll(high, fields, 1))
        per = plan.lab_rows // 8
        for part in range(per):
            gathered = jnp.zeros((8, LANES), jnp.float32)
            for group in range(plan.groups):
                tile = group * per + part
                if tile * 8 < plan.cap:
                    piece = rows_out[pl.ds(pl.multiple_of(start + tile * 8, 8), 8), :]
                    moved = pltpu.roll(piece, (group * LABELS - fields) % LANES, 1)
                    gathered = jnp.where(lane // LABELS == group, moved, gathered)
            packed[peer, pl.ds(plan.half + part * 8, 8), :] = gathered
        pltpu.make_async_copy(packed.at[peer], out_ref.at[peer], out_sems.at[peer]).start()
        return carry

    lax.fori_loop(0, peers, squeeze, 0)
    for peer in range(peers):
        pltpu.make_async_copy(packed.at[peer], out_ref.at[peer], out_sems.at[peer]).wait()


def partner(me, step, peers):
    if peers & (peers - 1):
        return lax.rem(me + step, peers)
    other, bit = jnp.int32(0), 1
    while bit < peers:
        mine = lax.rem(lax.div(me, jnp.int32(bit)), jnp.int32(2))
        other = other + bit * (1 - mine if step & bit else mine)
        bit *= 2
    return other


def exchange_kernel(plan, n_ha, send_ref, arrived_hbm, labels_hbm, got_ref, arrived_ref,
                    labels_ref, send_sem, recv_sem, own_sem, out_sems):
    fields, peers = plan.fields, plan.peers
    me = lax.axis_index("sa") * n_ha + lax.axis_index("ha")
    barrier = pltpu.get_barrier_semaphore()

    def where_is(peer):
        return {"sa": lax.div(peer, jnp.int32(n_ha)), "ha": lax.rem(peer, jnp.int32(n_ha))}

    others = [partner(me, step, peers) for step in range(1, peers)]
    for peer in others:
        pl.semaphore_signal(barrier, inc=1, device_id=where_is(peer),
                            device_id_type=pl.DeviceIdType.MESH)
    pl.semaphore_wait(barrier, peers - 1)
    copies = []
    for step, peer in enumerate(others, 1):
        copy = pltpu.make_async_remote_copy(
            src_ref=send_ref.at[peer],
            dst_ref=got_ref.at[step],
            send_sem=send_sem.at[step],
            recv_sem=recv_sem.at[step],
            device_id=where_is(peer),
            device_id_type=pl.DeviceIdType.MESH,
        )
        copy.start()
        copies.append(copy)
    own = pltpu.make_async_copy(send_ref.at[me], got_ref.at[0], own_sem)
    own.start()
    own.wait()

    per = plan.lab_rows // 8
    lane = lax.broadcasted_iota(jnp.int32, (8, LANES), 1)
    in_labels = (lane >= fields) & (lane < fields + LABELS)

    def spread(step):
        start = step * plan.cap
        for tile in range(plan.cap // 8):
            side, at = tile // (plan.half // 8), tile % (plan.half // 8)
            record = got_ref[step, pl.ds(at * 8, 8), :]
            group, part = tile // per, tile % per
            label = got_ref[step, pl.ds(plan.half + part * 8, 8), :]
            label = pltpu.roll(label, (fields - group * LABELS) % LANES, 1)
            if side:
                record = pltpu.roll(record, fields, 1)
            arrived_ref[pl.ds(pl.multiple_of(start + tile * 8, 8), 8), :] = jnp.where(
                lane < fields, record, jnp.where(in_labels, label, 0.0))
        put(step).start()

    def put(step):
        here = pl.ds(pl.multiple_of(step * plan.cap, 8), plan.cap)
        return pltpu.make_async_copy(
            arrived_ref.at[here, :], arrived_hbm.at[here, :], out_sems.at[step])

    spread(0)
    peer_of = others[0]

    def arrive(step, carry):
        pltpu.make_async_remote_copy(
            src_ref=send_ref.at[0], dst_ref=got_ref.at[step],
            send_sem=send_sem.at[step], recv_sem=recv_sem.at[step],
            device_id=where_is(peer_of), device_id_type=pl.DeviceIdType.MESH,
        ).wait_recv()
        spread(step)
        return carry

    lax.fori_loop(1, peers, arrive, 0)
    for tile in range(plan.lab_tiles):
        first = tile * plan.per_tile
        count = min(plan.per_tile, peers - first)
        pieces = [got_ref[first + k, pl.ds(plan.half, plan.lab_rows), :] for k in range(count)]
        rest = LANES - count * plan.lab_rows
        if rest:
            pieces.append(jnp.zeros((rest, LANES), jnp.float32))
        labels_ref[tile] = jnp.concatenate(pieces, axis=0).T.astype(jnp.int32)
    put_labels = pltpu.make_async_copy(labels_ref, labels_hbm, out_sems.at[peers])
    put_labels.start()
    for copy in copies:
        copy.wait_send()
    for step in range(peers):
        put(step).wait()
    put_labels.wait()


def unpack_kernel(plan, arrived_hbm, labels, blocks_ref, mass_ref, fmass_ref, mean_ref,
                  second_ref, arrived, placed, member_s, value_s, labels_s, sem, in_sems):
    fields, peers = plan.fields, plan.peers

    def take(step):
        here = pl.ds(pl.multiple_of(step * plan.cap, 8), plan.cap)
        return pltpu.make_async_copy(
            arrived_hbm.at[here, :], arrived.at[here, :], in_sems.at[step])

    copy = pltpu.make_async_copy(labels, labels_s, sem)
    copy.start()
    for step in range(peers):
        take(step).start()

    def clear(step, carry):
        for part in range(8):
            placed[pl.ds(pl.multiple_of(step * 64 + part * 8, 8), 8), :] = jnp.zeros(
                (8, LANES), jnp.float32)
        return carry

    lax.fori_loop(0, plan.slots // 64, clear, 0)
    copy.wait()

    for peer in range(peers):
        tile, offset = peer // plan.per_tile, peer % plan.per_tile * plan.lab_rows
        together = 3
        trips = plan.cap // (together * plan.lab_rows)

        def scatter(trip, carry, count=together * plan.lab_rows, peer=peer, tile=tile,
                    offset=offset):
            first = trip * together
            for rank in range(count):
                group, row = rank // plan.lab_rows, rank % plan.lab_rows
                to = labels_s[tile, (first + group) * LABELS + 1, offset + row]
                placed[pl.ds(to, 1), :] = arrived[
                    pl.ds(peer * plan.cap + first * plan.lab_rows + rank, 1), :]
            return carry

        take(peer).wait()
        lax.fori_loop(0, trips, scatter, 0)
        rest = plan.cap - trips * together * plan.lab_rows
        if rest:
            scatter(trips, 0, count=rest)

    total = jnp.zeros((1, 1), jnp.float32)
    for peer in range(peers):
        total = total + arrived[pl.ds(peer * plan.cap, 1), :][:, fields + 3:fields + 4]
    forests = lax.broadcasted_iota(jnp.int32, (FOR_DEV, LANES), 0).astype(jnp.float32)
    wide = lax.broadcasted_iota(jnp.int32, (LANES, LANES), 1)

    weights = jnp.zeros((FOR_DEV, LANES), jnp.float32)
    span = 4

    def some_blocks(part, weights):
        for inner in range(span):
            block = part * span + inner
            rows = placed[pl.ds(pl.multiple_of(block * LANES, LANES), LANES), :]
            turned = rows.T
            blocks_ref[pl.ds(block, fields, stride=BLK_DEV), :] = turned[:fields]
            mass_row = turned[fields:fields + 1]
            mass_ref[pl.ds(block, 1), :] = mass_row
            hit = turned[fields + 2:fields + 3] == forests
            weights = weights + jnp.where(hit, mass_row, 0.0)
            member_s[part, :, inner * LANES:(inner + 1) * LANES] = jnp.where(
                hit, 1.0, 0.0).astype(jnp.bfloat16)
            mass = rows[:, fields:fields + 1]
            value = jnp.where(wide < fields, rows, pltpu.roll(rows, fields, 1))
            scaled = mass * value
            scaled = jnp.where(wide < fields, scaled, scaled * value)
            high = scaled.astype(jnp.bfloat16)
            low = (scaled - high.astype(jnp.float32)).astype(jnp.bfloat16)
            here = pl.ds(inner * LANES, LANES)
            value_s[part, here, :LANES] = high
            value_s[part, here, LANES:] = low
        return weights

    weights = lax.fori_loop(0, BLK_DEV // span, some_blocks, weights)
    sums = jnp.zeros((FOR_DEV, 2 * LANES), jnp.float32)
    for part in range(BLK_DEV // span):
        sums = sums + jnp.dot(member_s[part], value_s[part], preferred_element_type=jnp.float32)
    sums = sums[:, :LANES] + sums[:, LANES:]
    weight = jnp.sum(weights.T, axis=0, keepdims=True)
    sums = sums.T
    fmass_ref[...] = weight * (float(FOR_DEV * peers) / total)
    mean_ref[...] = sums[:fields] / weight
    second_ref[...] = sums[fields:] / weight


def on_device(n_ha, peers, records, halo_mass, forest_id, dest_block, dest_slot):
    fields, snaps, halos = records.shape
    plan = Plan(fields, snaps, halos, peers)
    f32, i32 = jnp.float32, jnp.int32
    hbm = pl.BlockSpec(memory_space=pltpu.HBM)
    vmem = pl.BlockSpec(memory_space=pltpu.VMEM)
    full = pltpu.CompilerParams(vmem_limit_bytes=67043328)
    send = pl.pallas_call(
        functools.partial(pack_kernel, plan),
        out_shape=jax.ShapeDtypeStruct((peers, plan.rows, LANES), f32),
        in_specs=[hbm] * 5,
        out_specs=hbm,
        scratch_shapes=[
            pltpu.VMEM(records.shape, f32),
            pltpu.VMEM((snaps, halos), f32),
            pltpu.VMEM((snaps, halos), i32),
            pltpu.VMEM((snaps, halos), i32),
            pltpu.VMEM((snaps, halos), i32),
            pltpu.VMEM((plan.local, LANES), f32),
            pltpu.VMEM((peers * plan.cap, LANES), f32),
            pltpu.VMEM((peers, plan.rows, LANES), f32),
            pltpu.VMEM((4, plan.tiles, LANES), f32),
            pltpu.VMEM((peers * plan.tiles, LANES), jnp.bfloat16),
            pltpu.VMEM((plan.tiles, LANES), i32),
            pltpu.SMEM((plan.tiles, LANES), i32),
            pltpu.SemaphoreType.DMA,
            pltpu.SemaphoreType.DMA((5,)),
            pltpu.SemaphoreType.DMA((peers,)),
        ],
        compiler_params=full,
        name="pack",
    )(records, halo_mass, forest_id, dest_block, dest_slot)
    arrived, labels = pl.pallas_call(
        functools.partial(exchange_kernel, plan, n_ha),
        out_shape=(
            jax.ShapeDtypeStruct((peers * plan.cap, LANES), f32),
            jax.ShapeDtypeStruct((plan.lab_tiles, LANES, LANES), i32),
        ),
        in_specs=[hbm],
        out_specs=(hbm, hbm),
        scratch_shapes=[
            pltpu.VMEM(send.shape, f32),
            pltpu.VMEM((peers * plan.cap, LANES), f32),
            pltpu.VMEM((plan.lab_tiles, LANES, LANES), i32),
            pltpu.SemaphoreType.DMA((peers,)),
            pltpu.SemaphoreType.DMA((peers,)),
            pltpu.SemaphoreType.DMA,
            pltpu.SemaphoreType.DMA((peers + 1,)),
        ],
        compiler_params=pltpu.CompilerParams(
            collective_id=0, has_side_effects=True, vmem_limit_bytes=67043328),
        name="exchange",
    )(send)
    blocks, block_mass, forest_mass, mean, second = pl.pallas_call(
        functools.partial(unpack_kernel, plan),
        out_shape=(
            jax.ShapeDtypeStruct((fields * BLK_DEV, LANES), f32),
            jax.ShapeDtypeStruct((BLK_DEV, LANES), f32),
            jax.ShapeDtypeStruct((1, FOR_DEV), f32),
            jax.ShapeDtypeStruct((fields, FOR_DEV), f32),
            jax.ShapeDtypeStruct((fields, FOR_DEV), f32),
        ),
        in_specs=[hbm, hbm],
        out_specs=(vmem,) * 5,
        scratch_shapes=[
            pltpu.VMEM((peers * plan.cap, LANES), f32),
            pltpu.VMEM((plan.slots + 8, LANES), f32),
            pltpu.VMEM((10, FOR_DEV, 4 * LANES), jnp.bfloat16),
            pltpu.VMEM((10, 4 * LANES, 2 * LANES), jnp.bfloat16),
            pltpu.SMEM((plan.lab_tiles, LANES, LANES), i32),
            pltpu.SemaphoreType.DMA,
            pltpu.SemaphoreType.DMA((peers,)),
        ],
        compiler_params=full,
        name="unpack",
    )(arrived, labels)
    return (
        blocks.reshape(fields, BLK_DEV, LANES),
        block_mass,
        forest_mass.reshape(FOR_DEV),
        mean,
        second,
    )


def solution(mesh):
    n_ha = mesh.shape["ha"]
    peers = mesh.shape["sa"] * n_ha
    in_specs = (
        P(None, "sa", ("row", "ha")),
        P("sa", ("row", "ha")),
        P("sa", ("row", "ha")),
        P("sa", ("row", "ha")),
        P("sa", ("row", "ha")),
    )
    out_specs = (
        P(None, ("row", "sa", "ha"), None),
        P(("row", "sa", "ha"), None),
        P(("row", "sa", "ha")),
        P(None, ("row", "sa", "ha")),
        P(None, ("row", "sa", "ha")),
    )
    return jax.shard_map(
        functools.partial(on_device, n_ha, peers),
        mesh=mesh, in_specs=in_specs, out_specs=out_specs, check_vma=False
    )
```
